32 devices in a mesh: row: 8 (over y, x, core), col: 4 (over z).
Axes of the slice: x: 2, y: 2, z: 4, core: 2. Of those that a mesh axis runs over, the one named last changes fastest.
Arguments:
- a_blocks: bfloat16 [8, 4, 64, 128, 128], P('row', 'col'), may hold values from -6 to 6
- b_blocks: bfloat16 [8, 4, 2, 24, 128, 128], P('row', 'col'), may hold values from -0.1796875 to 0.1796875
- a_index: int32 [8, 4, 8, 192], P('row', 'col'), may hold values from 0 to 63
- b_index: int32 [8, 4, 8, 192], P('row', 'col'), may hold values from 0 to 23
- c_index: int32 [8, 4, 8, 192], P('row', 'col'), may hold values from 0 to 63
- pair_count: int32 [8, 4, 8], P('row', 'col'), may hold values from 1 to 192, as said below
Outputs:
- c_blocks: bfloat16 [8, 4, 64, 128, 128], P('row', 'col')
The draws below stay inside these ranges and needn't reach their ends.
Inputs may be any that keep to these rules, and one draw needn't show every extreme that they name: Only the first pair_count entries of each list are used; in every tick some C panel has all 192 entries live.
All inputs are finite; a program needn't handle non-finite values.
Results may differ from the reference program's by a relative error of at most 0.008.
Values may be sent and summed in bfloat16 or wider, within the bound.
No kernel may reach another device: no remote copies, remote signals or barrier semaphores. Data moves between devices by JAX's collectives and lax.ppermute only.
A program may use at most 192 MiB of HBM per device.

```python
import jax
import jax.numpy as jnp
from jax import lax

BS = 128
SLOTS_A = 64
SLOTS_B = 24
PAIRS = 192
SLOTS_C = 64
TICKS = 8
LOW = 3
HALVES = 2
N_ROW = 8
N_COL = 4


def draw_pair_count(key, part):
    first_key = jax.random.fold_in(key, 11)
    second_key = jax.random.fold_in(key, 23)
    busy_key = jax.random.fold_in(key, 37)
    shape = (N_ROW, N_COL, TICKS)
    first = jax.random.randint(first_key, shape, 1, PAIRS + 1)
    second = jax.random.randint(second_key, shape, 1, PAIRS + 1)
    counts = jnp.maximum(first * second // PAIRS, 1)
    busy = jax.random.randint(busy_key, (TICKS,), 0, N_ROW * N_COL)
    flat = jnp.arange(N_ROW * N_COL, dtype=jnp.int32).reshape(N_ROW, N_COL, 1)
    counts = jnp.where(flat == busy[None, None, :], PAIRS, counts)
    return counts.astype(jnp.int32)


def touch_ends(array, rng, smallest, largest):
    dims = array.shape
    index_at = [jax.random.randint(jax.random.fold_in(rng, axis), (), 0, dims[axis]) for axis in range(len(dims))]
    array = array.at[tuple(index_at)].set(smallest)
    longest = dims.index(max(dims))
    index_at[longest] = (index_at[longest] + 1) % dims[longest]
    return array.at[tuple(index_at)].set(largest)


def levels(rng, dims, cuts, least, high):
    loudness = 1.0
    for dim, shards_of in cuts:
        draws = jax.random.uniform(jax.random.fold_in(jax.random.fold_in(rng, 6), dim), (shards_of,), jnp.float32, least / len(cuts), high / len(cuts))
        loudness = loudness * jnp.repeat(jnp.exp(draws), dims[dim] // shards_of).reshape((-1,) + (1,) * (len(dims) - 1 - dim))
    return loudness


def scatter_about(stream_key, extent, scale, reach, split=(), kind=jnp.bfloat16):
    entries = scale * jax.random.normal(stream_key, extent, jnp.float32)
    if split:
        entries = entries * levels(stream_key, extent, split, -0.22, 0.18)
    return jnp.clip(entries, -reach, reach).astype(kind)


def setup_inputs(seed: int = 0) -> dict:
    streams_of = jax.random.split(jax.random.key(seed), 7)
    a_blocks = scatter_about(streams_of[0], (N_ROW, N_COL, SLOTS_A, BS, BS), 1.0, 6.0, ((0, 8), (1, 4)))
    b_blocks = scatter_about(streams_of[1], (N_ROW, N_COL, HALVES, SLOTS_B, BS, BS), 0.03, 0.1796875, ((0, 8), (1, 4)))
    a_index = touch_ends(jax.random.randint(streams_of[2], (N_ROW, N_COL, TICKS, PAIRS), 0, SLOTS_A), jax.random.fold_in(streams_of[2], 1), 0, SLOTS_A - 1).astype(jnp.int32)
    b_index = touch_ends(jax.random.randint(streams_of[3], (N_ROW, N_COL, TICKS, PAIRS), 0, SLOTS_B), jax.random.fold_in(streams_of[3], 1), 0, SLOTS_B - 1).astype(jnp.int32)
    c_index = touch_ends(jax.random.randint(streams_of[4], (N_ROW, N_COL, TICKS, PAIRS), 0, SLOTS_C), jax.random.fold_in(streams_of[4], 1), 0, SLOTS_C - 1).astype(jnp.int32)
    pair_count = draw_pair_count(jax.random.fold_in(streams_of[6], 71), 0)
    return {"a_blocks": a_blocks, "b_blocks": b_blocks, "a_index": a_index, "b_index": b_index, "c_index": c_index, "pair_count": pair_count}


def panel_blocks(a_blocks, b_blocks, a_index, b_index, c_index, pair_count, row_index, col_index):
    running = jnp.zeros((SLOTS_C, BS, BS), jnp.float32)
    positions = jnp.arange(PAIRS, dtype=jnp.int32)
    for tick in range(TICKS):
        offset = tick - LOW
        a_panel = a_blocks[(row_index + offset) % N_ROW, col_index]
        half_index = ((row_index + col_index + offset) % N_ROW) // N_COL
        b_panel = b_blocks[row_index, (col_index + offset) % N_COL, half_index]
        a_rows = a_panel[a_index[row_index, col_index, tick]].astype(jnp.float32)
        b_rows = b_panel[b_index[row_index, col_index, tick]].astype(jnp.float32)
        products = jnp.einsum("pik,pjk->pij", a_rows, b_rows)
        live_mask = (positions < pair_count[row_index, col_index, tick]).astype(jnp.float32)
        running = running.at[c_index[row_index, col_index, tick]].add(products * live_mask[:, None, None])
    return running.astype(jnp.bfloat16)


def reference(a_blocks, b_blocks, a_index, b_index, c_index, pair_count):
    devices = jnp.arange(N_ROW * N_COL, dtype=jnp.int32)

    def one_panel(device):
        return panel_blocks(a_blocks, b_blocks, a_index, b_index, c_index, pair_count, device // N_COL, device % N_COL)

    result = lax.map(one_panel, devices)
    return result.reshape(N_ROW, N_COL, SLOTS_C, BS, BS)
```

```python
import functools

import jax
import jax.numpy as jnp
import numpy as np
from jax import lax
from jax.experimental import pallas as pl
from jax.experimental.pallas import tpu as pltpu
from jax.sharding import PartitionSpec as P

SLOTS_C = 64
GROUP = 16
FIELDS = 32
B_SHIFT, C_SHIFT = 8, 16
HBM = pl.BlockSpec(memory_space=pltpu.HBM)


def stage_kernel(table, counts, packed, *refs, stage, a_views, b_views, n_inputs, first, last):
    inputs = refs[:n_inputs]
    rest = refs[n_inputs:]
    c_in, rest = (None, rest) if first else (rest[0], rest[1:])
    out, total, a_buf, b_buf, b_turned, a_sem, b_sem, c_sem = rest[:8]
    rounded = rest[8] if last else None
    base = stage * FIELDS
    entries = table[base]
    slots_c = SLOTS_C

    def fetch(k, slot):
        a_id = table[base + 2 + 3 * k]
        b_id = table[base + 3 + 3 * k]
        for number, pieces in enumerate(a_views):

            @pl.when(a_id == number)
            def _(pieces=pieces):
                for ref_number, offset, size in pieces:
                    pltpu.make_async_copy(
                        inputs[ref_number], a_buf.at[slot, pl.ds(offset, size)], a_sem.at[slot]
                    ).start()

        for number, (ref_number, half) in enumerate(b_views):

            @pl.when(b_id == number)
            def _(ref_number=ref_number, half=half):
                source = inputs[ref_number] if half is None else inputs[ref_number].at[half]
                pltpu.make_async_copy(source, b_buf.at[slot], b_sem.at[slot]).start()

    def await_fetch(slot):
        pltpu.make_async_copy(a_buf.at[slot], a_buf.at[slot], a_sem.at[slot]).wait()
        pltpu.make_async_copy(b_buf.at[slot], b_buf.at[slot], b_sem.at[slot]).wait()

    if not first:
        brought = pltpu.make_async_copy(c_in, total.at[pl.ds(0, slots_c)], c_sem.at[0])
        brought.start()

    @pl.when(entries > 0)
    def _():
        fetch(0, 0)

    if first:
        total[...] = jnp.zeros_like(total)
    else:
        total[pl.ds(slots_c, 1)] = jnp.zeros_like(total[pl.ds(slots_c, 1)])
        brought.wait()

    def one_tick(k, carry):
        slot = lax.rem(k, 2)
        await_fetch(slot)

        @pl.when(k + 1 < entries)
        def _():
            fetch(k + 1, 1 - slot)

        tick = table[base + 1 + 3 * k]
        for s in range(b_buf.shape[1]):
            b_turned[s] = b_buf[slot, s].T

        def one_group(g, carry):
            for u in range(GROUP):
                word = packed[tick, g * GROUP + u]
                a_at = word & 255
                b_at = (word >> B_SHIFT) & 255
                c_at = word >> C_SHIFT
                product = jnp.dot(a_buf[slot, a_at], b_turned[b_at], preferred_element_type=jnp.float32)
                total[c_at] = total[c_at] + product
            return carry

        lax.fori_loop(0, (counts[tick] + GROUP - 1) // GROUP, one_group, 0)
        return carry

    lax.fori_loop(0, entries, one_tick, 0)

    if last:
        chunk = 16
        copies = []
        for start in range(0, slots_c, chunk):
            part = pl.ds(start, chunk)
            rounded[part] = total[part].astype(jnp.bfloat16)
            copies.append(pltpu.make_async_copy(rounded.at[part], out.at[part], c_sem.at[start // chunk]))
            copies[-1].start()
        for copy in copies:
            copy.wait()
    else:
        done = pltpu.make_async_copy(total.at[pl.ds(0, slots_c)], out, c_sem.at[0])
        done.start()
        done.wait()


def run_stage(stage, table, counts, packed, arrays, a_views, b_views, c_in, last, pairs_hint):
    first = c_in is None
    slots_a = max(sum(piece[2] for piece in pieces) for pieces in a_views)
    slots_b, bs = arrays[b_views[0][0]].shape[-3:-1]
    operands = list(arrays) + ([] if first else [c_in])
    kernel = functools.partial(
        stage_kernel,
        stage=stage,
        a_views=a_views,
        b_views=b_views,
        n_inputs=len(arrays),
        first=first,
        last=last,
    )
    scratch = [
        pltpu.VMEM((SLOTS_C + 1, bs, bs), jnp.float32),
        pltpu.VMEM((2, slots_a, bs, bs), jnp.bfloat16),
        pltpu.VMEM((2, slots_b, bs, bs), jnp.bfloat16),
        pltpu.VMEM((slots_b, bs, bs), jnp.bfloat16),
        pltpu.SemaphoreType.DMA((2,)),
        pltpu.SemaphoreType.DMA((2,)),
        pltpu.SemaphoreType.DMA((4,)),
    ]
    if last:
        scratch.append(pltpu.VMEM((SLOTS_C, bs, bs), jnp.bfloat16))
    return pl.pallas_call(
        kernel,
        out_shape=jax.ShapeDtypeStruct((SLOTS_C, bs, bs), jnp.bfloat16 if last else jnp.float32),
        grid_spec=pltpu.PrefetchScalarGridSpec(
            num_scalar_prefetch=3,
            grid=(1,),
            in_specs=[HBM] * len(operands),
            out_specs=HBM,
            scratch_shapes=scratch,
        ),
        compiler_params=pltpu.CompilerParams(vmem_limit_bytes=32 << 20),
        cost_estimate=pl.CostEstimate(
            flops=2 * bs**3 * pairs_hint, bytes_accessed=16 << 20, transcendentals=0
        ),
        name=f"stage{stage}",
    )(table, counts, packed, *operands)


def packed_lists(a_index, b_index, c_index, pair_count):
    position = lax.broadcasted_iota(jnp.int32, a_index.shape, 1)
    target = jnp.where(position < pair_count[:, None], c_index, SLOTS_C)
    return a_index | (b_index << B_SHIFT) | (target << C_SHIFT)


def shifted(value, axis, steps):
    count = lax.axis_size(axis)
    return lax.ppermute(value, axis, [(source, (source + steps) % count) for source in range(count)])


def any_mesh(a_blocks, b_blocks, a_index, b_index, c_index, pair_count):
    row, col = lax.axis_index("row"), lax.axis_index("col")
    rows, cols = lax.axis_size("row"), lax.axis_size("col")
    ticks = a_index.shape[2]
    back = ticks // 2 - 1
    counts = pair_count[0, 0]
    packed = packed_lists(a_index[0, 0], b_index[0, 0], c_index[0, 0], counts)
    a_now = shifted(a_blocks[0, 0], "row", back)
    b_now = shifted(b_blocks[0, 0], "col", back)
    halves = b_now.shape[0]
    running = None
    for tick in range(ticks):
        half = (row + col + tick - back) % rows // cols
        entry = jnp.concatenate(
            [jnp.array([1, tick, 0], jnp.int32), half[None].astype(jnp.int32), jnp.zeros((FIELDS - 4,), jnp.int32)]
        )
        running = run_stage(
            0, entry, counts, packed, [a_now, b_now],
            [[(0, 0, a_now.shape[0])]], [(1, h) for h in range(halves)],
            running, tick == ticks - 1, packed.shape[1],
        )
        if tick < ticks - 1:
            a_now = shifted(a_now, "row", -1)
            b_now = shifted(b_now, "col", -1)
    return running[None, None]


OWN, OUTER, INNER, SECOND, INNER_FAR, THIRD = range(6)


def b_source(col, target):
    if target == col:
        return OWN
    if col in (0, 3):
        return (None, OUTER, SECOND, THIRD)[abs(target - col)]
    if abs(target - col) == 2:
        return INNER_FAR
    return OUTER if target in (0, 3) else INNER


def stage_tables(stage_of, n_stages, rows=8, cols=4, ticks=8):
    tables = np.zeros((rows, cols, n_stages, FIELDS), np.int32)
    for row in range(rows):
        for col in range(cols):
            lists = [[] for _ in range(n_stages)]
            for tick in range(ticks):
                offset = tick - (ticks // 2 - 1)
                a_id = row ^ ((row + offset) % rows)
                source = b_source(col, (col + offset) % cols)
                half = (row + col + offset) % rows // cols
                lists[stage_of(a_id, source, half)].append((tick, a_id, 2 * source + half))
            for stage, entries in enumerate(lists):
                tables[row, col, stage, 0] = len(entries)
                for k, entry in enumerate(entries):
                    tables[row, col, stage, 1 + 3 * k : 4 + 3 * k] = entry
    return tables


def gather_b(b_own):
    outer_both, inner_both, outward = [(0, 1), (1, 0), (2, 3), (3, 2)], [(1, 2), (2, 1)], [(1, 0), (2, 3)]
    streams = []
    for half in range(2):
        own = b_own[half]
        outer = lax.ppermute(own, "col", outer_both)
        inner = lax.ppermute(own, "col", inner_both)
        second = lax.ppermute(inner, "col", outward)
        inner_far = lax.ppermute(outer, "col", inner_both)
        third = lax.ppermute(inner_far, "col", outward)
        streams.append((outer, inner, second, inner_far, third))
    return streams


def across(value, bit):
    return lax.ppermute(value, "row", [(source, source ^ bit) for source in range(8)])


def block_mesh(a_blocks, b_blocks, a_index, b_index, c_index, pair_count):
    row, col = lax.axis_index("row"), lax.axis_index("col")
    counts = pair_count[0, 0]
    packed = packed_lists(a_index[0, 0], b_index[0, 0], c_index[0, 0], counts)
    table = jnp.asarray(stage_tables(lambda a, b, h: 0, 1))[row, col].reshape(-1)
    a_own, b_own = a_blocks[0, 0], b_blocks[0, 0]
    cut = a_own.shape[0] // 2
    streams = gather_b(b_own)
    a_x, a_y = across(a_own, 2), across(a_own, 4)
    a_d = (across(a_y[:cut], 2), across(a_x[cut:], 4))
    own_chip = [a_own, a_x, a_y, *a_d]
    arrays = own_chip + [across(value, 1) for value in own_chip] + [b_own]
    slots = a_own.shape[0]
    whole = lambda number: [(number, 0, slots)]
    split = lambda number: [(number, 0, cut), (number + 1, cut, slots - cut)]
    a_views = [whole(0), whole(5), whole(1), whole(6), whole(2), whole(7), split(3), split(8)]
    b_views = [(10, 0), (10, 1)]
    for hop in range(5):
        for half in range(2):
            b_views.append((len(arrays), None))
            arrays.append(streams[half][hop])
    total = run_stage(0, table, counts, packed, arrays, a_views, b_views, None, True, 8 * packed.shape[1])
    return total[None, None]


def solution(mesh):
    placed = (
        P("row", "col", None, None, None),
        P("row", "col", None, None, None, None),
        P("row", "col", None, None),
        P("row", "col", None, None),
        P("row", "col", None, None),
        P("row", "col", None),
    )
    exact = (mesh.shape["row"], mesh.shape["col"]) == (8, 4)
    return jax.shard_map(
        block_mesh if exact else any_mesh,
        mesh=mesh,
        in_specs=placed,
        out_specs=P("row", "col", None, None, None),
        check_vma=False,
    )
```

```python
import functools

import jax
import jax.numpy as jnp
import numpy as np
from jax import lax
from jax.experimental import pallas as pl
from jax.experimental.pallas import tpu as pltpu
from jax.sharding import PartitionSpec as P

SLOTS_C = 64
GROUP = 16
FIELDS = 32
B_SHIFT, C_SHIFT = 8, 16
HBM = pl.BlockSpec(memory_space=pltpu.HBM)


def stage_kernel(table, counts, packed, *refs, stage, a_views, b_views, n_inputs, first, last):
    inputs = refs[:n_inputs]
    rest = refs[n_inputs:]
    c_in, rest = (None, rest) if first else (rest[0], rest[1:])
    out, total, a_buf, b_buf, b_turned, a_sem, b_sem, c_sem = rest[:8]
    rounded = rest[8] if last else None
    base = stage * FIELDS
    entries = table[base]
    slots_c = SLOTS_C

    def fetch(k, slot):
        a_id = table[base + 2 + 3 * k]
        b_id = table[base + 3 + 3 * k]
        for number, pieces in a_views.items():

            @pl.when(a_id == number)
            def _(pieces=pieces):
                size = a_buf.shape[1] // len(pieces)
                for piece, ref_number in enumerate(pieces):
                    target = a_buf.at[slot, pl.ds(piece * size, size)]
                    pltpu.make_async_copy(inputs[ref_number], target, a_sem.at[slot]).start()

        for number, (ref_number, half) in b_views.items():

            @pl.when(b_id == number)
            def _(ref_number=ref_number, half=half):
                source = inputs[ref_number] if half is None else inputs[ref_number].at[half]
                pltpu.make_async_copy(source, b_buf.at[slot], b_sem.at[slot]).start()

    def await_fetch(slot):
        pltpu.make_async_copy(a_buf.at[slot], a_buf.at[slot], a_sem.at[slot]).wait()
        pltpu.make_async_copy(b_buf.at[slot], b_buf.at[slot], b_sem.at[slot]).wait()

    if not first:
        brought = pltpu.make_async_copy(c_in, total.at[pl.ds(0, slots_c)], c_sem.at[0])
        brought.start()

    @pl.when(entries > 0)
    def _():
        fetch(0, 0)

    if first:
        total[...] = jnp.zeros_like(total)
    else:
        total[pl.ds(slots_c, 1)] = jnp.zeros_like(total[pl.ds(slots_c, 1)])
        brought.wait()

    def one_tick(k, carry):
        slot = lax.rem(k, 2)
        await_fetch(slot)

        @pl.when(k + 1 < entries)
        def _():
            fetch(k + 1, 1 - slot)

        tick = table[base + 1 + 3 * k]
        for s in range(b_buf.shape[1]):
            b_turned[s] = b_buf[slot, s].T

        def one_group(g, carry):
            for u in range(GROUP):
                word = packed[tick, g * GROUP + u]
                a_at = word & 255
                b_at = (word >> B_SHIFT) & 255
                c_at = word >> C_SHIFT
                product = jnp.dot(a_buf[slot, a_at], b_turned[b_at], preferred_element_type=jnp.float32)
                total[c_at] = total[c_at] + product
            return carry

        lax.fori_loop(0, (counts[tick] + GROUP - 1) // GROUP, one_group, 0)
        return carry

    lax.fori_loop(0, entries, one_tick, 0)

    if last:
        chunk = 16
        copies = []
        for start in range(0, slots_c, chunk):
            part = pl.ds(start, chunk)
            rounded[part] = total[part].astype(jnp.bfloat16)
            copies.append(pltpu.make_async_copy(rounded.at[part], out.at[part], c_sem.at[start // chunk]))
            copies[-1].start()
        for copy in copies:
            copy.wait()
    else:
        done = pltpu.make_async_copy(total.at[pl.ds(0, slots_c)], out, c_sem.at[0])
        done.start()
        done.wait()


def run_stage(stage, table, counts, packed, arrays, a_views, b_views, c_in, last, pairs_hint):
    first = c_in is None
    slots_a = sum(arrays[number].shape[0] for number in next(iter(a_views.values())))
    slots_b, bs = arrays[next(iter(b_views.values()))[0]].shape[-3:-1]
    operands = list(arrays) + ([] if first else [c_in])
    kernel = functools.partial(
        stage_kernel,
        stage=stage,
        a_views=a_views,
        b_views=b_views,
        n_inputs=len(arrays),
        first=first,
        last=last,
    )
    scratch = [
        pltpu.VMEM((SLOTS_C + 1, bs, bs), jnp.float32),
        pltpu.VMEM((2, slots_a, bs, bs), jnp.bfloat16),
        pltpu.VMEM((2, slots_b, bs, bs), jnp.bfloat16),
        pltpu.VMEM((slots_b, bs, bs), jnp.bfloat16),
        pltpu.SemaphoreType.DMA((2,)),
        pltpu.SemaphoreType.DMA((2,)),
        pltpu.SemaphoreType.DMA((4,)),
    ]
    if last:
        scratch.append(pltpu.VMEM((SLOTS_C, bs, bs), jnp.bfloat16))
    return pl.pallas_call(
        kernel,
        out_shape=jax.ShapeDtypeStruct((SLOTS_C, bs, bs), jnp.bfloat16 if last else jnp.float32),
        grid_spec=pltpu.PrefetchScalarGridSpec(
            num_scalar_prefetch=3,
            grid=(1,),
            in_specs=[HBM] * len(operands),
            out_specs=HBM,
            scratch_shapes=scratch,
        ),
        compiler_params=pltpu.CompilerParams(vmem_limit_bytes=60 << 20),
        cost_estimate=pl.CostEstimate(
            flops=0, bytes_accessed=0, transcendentals=0
        ),
        name=f"stage{stage}",
    )(table, counts, packed, *operands)


def packed_lists(a_index, b_index, c_index, pair_count):
    position = lax.broadcasted_iota(jnp.int32, a_index.shape, 1)
    target = jnp.where(position < pair_count[:, None], c_index, SLOTS_C)
    return a_index | (b_index << B_SHIFT) | (target << C_SHIFT)


def shifted(value, axis, steps):
    count = lax.axis_size(axis)
    return lax.ppermute(value, axis, [(source, (source + steps) % count) for source in range(count)])


def any_mesh(a_blocks, b_blocks, a_index, b_index, c_index, pair_count):
    row, col = lax.axis_index("row"), lax.axis_index("col")
    rows, cols = lax.axis_size("row"), lax.axis_size("col")
    ticks = a_index.shape[2]
    back = ticks // 2 - 1
    counts = pair_count[0, 0]
    packed = packed_lists(a_index[0, 0], b_index[0, 0], c_index[0, 0], counts)
    a_now = shifted(a_blocks[0, 0], "row", back)
    b_now = shifted(b_blocks[0, 0], "col", back)
    halves = b_now.shape[0]
    running = None
    for tick in range(ticks):
        half = (row + col + tick - back) % rows // cols
        entry = jnp.concatenate(
            [jnp.array([1, tick, 0], jnp.int32), half[None].astype(jnp.int32), jnp.zeros((FIELDS - 4,), jnp.int32)]
        )
        running = run_stage(
            0, entry, counts, packed, [a_now, b_now],
            {0: (0,)}, {h: (1, h) for h in range(halves)},
            running, tick == ticks - 1, packed.shape[1],
        )
        if tick < ticks - 1:
            a_now = shifted(a_now, "row", -1)
            b_now = shifted(b_now, "col", -1)
    return running[None, None]


ROWS, COLS = 8, 4
OWN, OUTER, INNER, SECOND, INNER_FAR, THIRD = range(6)
A_STAGE = (0, 0, 0, 0, 0, 0, 0, 0)
B_STAGE = ((0, 0), (0, 0), (0, 0), (0, 0), (0, 0), (0, 1))
STAGES = 2


def a_place(row, target):
    return row ^ target


def b_source(col, target):
    if target == col:
        return OWN
    if col in (0, 3):
        return (None, OUTER, SECOND, THIRD)[abs(target - col)]
    if abs(target - col) == 2:
        return INNER_FAR
    return OUTER if target in (0, 3) else INNER


def stage_tables(ticks=8):
    tables = np.zeros((ROWS, COLS, STAGES, FIELDS), np.int32)
    for row in range(ROWS):
        for col in range(COLS):
            lists = [[] for _ in range(STAGES)]
            for tick in range(ticks):
                offset = tick - (ticks // 2 - 1)
                place = a_place(row, (row + offset) % ROWS)
                source = b_source(col, (col + offset) % COLS)
                half = (row + col + offset) % ROWS // COLS
                ready = max(A_STAGE[place], B_STAGE[source][half])
                lists[ready].append((tick, place, 2 * source + half))
            for stage, entries in enumerate(lists):
                tables[row, col, stage, 0] = len(entries)
                for k, entry in enumerate(entries):
                    tables[row, col, stage, 1 + 3 * k : 4 + 3 * k] = entry
    return tables


def used(tables, stage, field):
    found = set()
    for entries in tables[:, :, stage].reshape(-1, FIELDS):
        found |= {int(entries[field + 3 * k]) for k in range(entries[0])}
    return sorted(found)


def sent(name, value, place_of):
    pairs = []
    for row in range(ROWS):
        for col in range(COLS):
            to_row, to_col = place_of(row, col)
            pairs.append((COLS * row + col, COLS * to_row + to_col))
    with jax.named_scope(name):
        return lax.ppermute(value, ("row", "col"), pairs)


def after(value, *others):
    return lax.optimization_barrier((value, *others))[0]


def outward(value, name):
    return sent(name, value, lambda row, col: (row, col ^ 1))


def inward(value, name):
    return sent(name, value, lambda row, col: (row, 3 - col) if col in (1, 2) else (row ^ 1, col))


def second_over(value, name):
    return sent(name, value, lambda row, col: (row ^ 1, (2, 0, 3, 1)[col]) if col in (0, 3) else (row, (2, 0, 3, 1)[col]))


def end_to_end(value, name):
    return sent(name, value, lambda row, col: (row, 3 - col) if col in (0, 3) else (row ^ 1, col))


def swapped(value, name):
    return sent(name, value, lambda row, col: (row ^ 1, col))


def across(value, bits, name):
    return sent(name, value, lambda row, col: (row ^ bits, col))


def block_mesh(a_blocks, b_blocks, a_index, b_index, c_index, pair_count):
    row, col = lax.axis_index("row"), lax.axis_index("col")
    counts = pair_count[0, 0]
    packed = packed_lists(a_index[0, 0], b_index[0, 0], c_index[0, 0], counts)
    tables = stage_tables(a_index.shape[2])
    table = jnp.asarray(tables)[row, col].reshape(-1)
    a_own, b_own = a_blocks[0, 0], b_blocks[0, 0]
    def stage_call(stage, total):
        arrays, a_views, b_views = [], {}, {}

        def number_of(value):
            for number, held in enumerate(arrays):
                if held is value:
                    return number
            arrays.append(value)
            return len(arrays) - 1

        for place in used(tables, stage, 2):
            a_views[place] = tuple(number_of(value) for value in a_at[place])
        for source in used(tables, stage, 3):
            value, half = b_at[source]
            b_views[source] = (number_of(value), half)
        return run_stage(stage, table, counts, packed, arrays, a_views, b_views, total, stage == STAGES - 1, 150)

    outer, inner, second_b, inner_far, third = [], [], [], [], []
    by_x, by_y = across(a_own, 2, "Ax"), across(a_own, 4, "Ay")
    cut = a_own.shape[0] // 2
    for half in range(2):
        outer.append(outward(b_own[half], f"O{half}"))
        inner.append(inward(b_own[half], f"I{half}"))
        second_b.append(outward(inner[half], f"S{half}"))
        inner_far.append(inward(outer[half], f"F{half}"))
        third.append(outward(inner_far[half], f"T{half}"))
    by_both = (across(by_y[:cut], 2, "Ad0"), across(by_x[cut:], 4, "Ad1"))
    on_chip = [(a_own,), (by_x,), (by_y,), by_both]
    a_at = []
    for number, pieces in enumerate(on_chip):
        a_at += [pieces, tuple(swapped(value, f"W{number}") for value in pieces)]
    b_at = [(b_own, 0), (b_own, 1)]
    for halves in (outer, inner, second_b, inner_far, third):
        b_at += [(value, None) for value in halves]
    total = None
    for stage in range(STAGES):
        total = stage_call(stage, total)

    return total[None, None]


def solution(mesh):
    placed = (
        P("row", "col", None, None, None),
        P("row", "col", None, None, None, None),
        P("row", "col", None, None),
        P("row", "col", None, None),
        P("row", "col", None, None),
        P("row", "col", None),
    )
    exact = (mesh.shape["row"], mesh.shape["col"]) == (ROWS, COLS)
    return jax.shard_map(
        block_mesh if exact else any_mesh,
        mesh=mesh,
        in_specs=placed,
        out_specs=P("row", "col", None, None, None),
        check_vma=False,
    )
```

```python
import functools

import jax
import jax.numpy as jnp
import numpy as np
from jax import lax
from jax.experimental import pallas as pl
from jax.experimental.pallas import tpu as pltpu
from jax.sharding import PartitionSpec as P

SLOTS_C = 64
GROUP = 32
BUFFERS = 3
FIELDS = 32
B_SHIFT, C_SHIFT = 8, 16
HBM = pl.BlockSpec(memory_space=pltpu.HBM)


def stage_kernel(table, counts, packed, *refs, stage, a_views, b_views, n_inputs, first, last):
    inputs = refs[:n_inputs]
    rest = refs[n_inputs:]
    c_in, rest = (None, rest) if first else (rest[0], rest[1:])
    out, total, a_buf, b_buf, b_turned, a_sem, b_sem, c_sem = rest[:8]
    rounded = rest[8] if last else None
    base = stage * FIELDS
    entries = table[base]
    slots_c = SLOTS_C

    def fetch(k, slot):
        a_id = table[base + 2 + 3 * k]
        b_id = table[base + 3 + 3 * k]
        for number, pieces in a_views.items():

            @pl.when(a_id == number)
            def _(pieces=pieces):
                size = a_buf.shape[1] // len(pieces)
                for piece, ref_number in enumerate(pieces):
                    target = a_buf.at[slot, pl.ds(piece * size, size)]
                    pltpu.make_async_copy(inputs[ref_number], target, a_sem.at[slot]).start()

        for number, (ref_number, half) in b_views.items():

            @pl.when(b_id == number)
            def _(ref_number=ref_number, half=half):
                source = inputs[ref_number] if half is None else inputs[ref_number].at[half]
                pltpu.make_async_copy(source, b_buf.at[slot], b_sem.at[slot]).start()

    def await_fetch(slot):
        pltpu.make_async_copy(a_buf.at[slot], a_buf.at[slot], a_sem.at[slot]).wait()
        pltpu.make_async_copy(b_buf.at[slot], b_buf.at[slot], b_sem.at[slot]).wait()

    if not first:
        brought = pltpu.make_async_copy(c_in, total.at[pl.ds(0, slots_c)], c_sem.at[0])
        brought.start()

    for ahead in range(BUFFERS - 1):

        @pl.when(ahead < entries)
        def _(ahead=ahead):
            fetch(ahead, ahead)

    if first:
        total[...] = jnp.zeros_like(total)
    else:
        total[pl.ds(slots_c, 1)] = jnp.zeros_like(total[pl.ds(slots_c, 1)])
        brought.wait()

    def one_tick(k, carry):
        slot = lax.rem(k, BUFFERS)
        await_fetch(slot)

        @pl.when(k + BUFFERS - 1 < entries)
        def _():
            fetch(k + BUFFERS - 1, lax.rem(k + BUFFERS - 1, BUFFERS))

        tick = table[base + 1 + 3 * k]
        for s in range(b_buf.shape[1]):
            b_turned[s] = b_buf[slot, s].T

        def one_group(g, carry):
            for u in range(GROUP):
                word = packed[tick, g * GROUP + u]
                a_at = word & 255
                b_at = (word >> B_SHIFT) & 255
                c_at = word >> C_SHIFT
                product = jnp.dot(a_buf[slot, a_at], b_turned[b_at], preferred_element_type=jnp.float32)
                total[c_at] = total[c_at] + product
            return carry

        lax.fori_loop(0, (counts[tick] + GROUP - 1) // GROUP, one_group, 0)
        return carry

    lax.fori_loop(0, entries, one_tick, 0)

    if last:
        chunk = 16
        copies = []
        for start in range(0, slots_c, chunk):
            part = pl.ds(start, chunk)
            rounded[part] = total[part].astype(jnp.bfloat16)
            copies.append(pltpu.make_async_copy(rounded.at[part], out.at[part], c_sem.at[start // chunk]))
            copies[-1].start()
        for copy in copies:
            copy.wait()
    else:
        done = pltpu.make_async_copy(total.at[pl.ds(0, slots_c)], out, c_sem.at[0])
        done.start()
        done.wait()


def run_stage(stage, table, counts, packed, arrays, a_views, b_views, c_in, last, pairs_hint):
    first = c_in is None
    slots_a = sum(arrays[number].shape[0] for number in next(iter(a_views.values())))
    slots_b, bs = arrays[next(iter(b_views.values()))[0]].shape[-3:-1]
    operands = list(arrays) + ([] if first else [c_in])
    kernel = functools.partial(
        stage_kernel,
        stage=stage,
        a_views=a_views,
        b_views=b_views,
        n_inputs=len(arrays),
        first=first,
        last=last,
    )
    scratch = [
        pltpu.VMEM((SLOTS_C + 1, bs, bs), jnp.float32),
        pltpu.VMEM((BUFFERS, slots_a, bs, bs), jnp.bfloat16),
        pltpu.VMEM((BUFFERS, slots_b, bs, bs), jnp.bfloat16),
        pltpu.VMEM((slots_b, bs, bs), jnp.bfloat16),
        pltpu.SemaphoreType.DMA((BUFFERS,)),
        pltpu.SemaphoreType.DMA((BUFFERS,)),
        pltpu.SemaphoreType.DMA((4,)),
    ]
    if last:
        scratch.append(pltpu.VMEM((SLOTS_C, bs, bs), jnp.bfloat16))
    return pl.pallas_call(
        kernel,
        out_shape=jax.ShapeDtypeStruct((SLOTS_C, bs, bs), jnp.bfloat16 if last else jnp.float32),
        grid_spec=pltpu.PrefetchScalarGridSpec(
            num_scalar_prefetch=3,
            grid=(1,),
            in_specs=[HBM] * len(operands),
            out_specs=HBM,
            scratch_shapes=scratch,
        ),
        compiler_params=pltpu.CompilerParams(vmem_limit_bytes=60 << 20),
        cost_estimate=pl.CostEstimate(
            flops=0, bytes_accessed=0, transcendentals=0
        ),
        name=f"stage{stage}",
    )(table, counts, packed, *operands)


def packed_lists(a_index, b_index, c_index, pair_count):
    position = lax.broadcasted_iota(jnp.int32, a_index.shape, 1)
    target = jnp.where(position < pair_count[:, None], c_index, SLOTS_C)
    return a_index | (b_index << B_SHIFT) | (target << C_SHIFT)


def shifted(value, axis, steps):
    count = lax.axis_size(axis)
    return lax.ppermute(value, axis, [(source, (source + steps) % count) for source in range(count)])


def any_mesh(a_blocks, b_blocks, a_index, b_index, c_index, pair_count):
    row, col = lax.axis_index("row"), lax.axis_index("col")
    rows, cols = lax.axis_size("row"), lax.axis_size("col")
    ticks = a_index.shape[2]
    back = ticks // 2 - 1
    counts = pair_count[0, 0]
    packed = packed_lists(a_index[0, 0], b_index[0, 0], c_index[0, 0], counts)
    a_now = shifted(a_blocks[0, 0], "row", back)
    b_now = shifted(b_blocks[0, 0], "col", back)
    halves = b_now.shape[0]
    running = None
    for tick in range(ticks):
        half = (row + col + tick - back) % rows // cols
        entry = jnp.concatenate(
            [jnp.array([1, tick, 0], jnp.int32), half[None].astype(jnp.int32), jnp.zeros((FIELDS - 4,), jnp.int32)]
        )
        running = run_stage(
            0, entry, counts, packed, [a_now, b_now],
            {0: (0,)}, {h: (1, h) for h in range(halves)},
            running, tick == ticks - 1, packed.shape[1],
        )
        if tick < ticks - 1:
            a_now = shifted(a_now, "row", -1)
            b_now = shifted(b_now, "col", -1)
    return running[None, None]


ROWS, COLS = 8, 4
OWN, OUTER, INNER, SECOND, INNER_FAR, THIRD = range(6)
A_STAGE = (0, 0, 0, 0, 0, 0, 0, 0)
B_STAGE = ((0, 0), (0, 0), (0, 0), (0, 0), (0, 0), (0, 1))
STAGES = 2


def a_place(row, target):
    delta = row ^ target
    by_core, hop = delta & 1, delta & 6
    if hop in (0, 6):
        return hop + by_core
    return (2 if (hop == 2) == ((row & 1) == by_core) else 4) + by_core


def b_source(col, target):
    if target == col:
        return OWN
    if col in (0, 3):
        return (None, OUTER, SECOND, THIRD)[abs(target - col)]
    if abs(target - col) == 2:
        return INNER_FAR
    return OUTER if target in (0, 3) else INNER


def stage_tables(ticks=8):
    tables = np.zeros((ROWS, COLS, STAGES, FIELDS), np.int32)
    for row in range(ROWS):
        for col in range(COLS):
            lists = [[] for _ in range(STAGES)]
            for tick in range(ticks):
                offset = tick - (ticks // 2 - 1)
                place = a_place(row, (row + offset) % ROWS)
                source = b_source(col, (col + offset) % COLS)
                half = (row + col + offset) % ROWS // COLS
                ready = max(A_STAGE[place], B_STAGE[source][half])
                lists[ready].append((tick, place, 2 * source + half))
            for stage, entries in enumerate(lists):
                tables[row, col, stage, 0] = len(entries)
                for k, entry in enumerate(entries):
                    tables[row, col, stage, 1 + 3 * k : 4 + 3 * k] = entry
    return tables


def used(tables, stage, field):
    found = set()
    for entries in tables[:, :, stage].reshape(-1, FIELDS):
        found |= {int(entries[field + 3 * k]) for k in range(entries[0])}
    return sorted(found)


def sent(name, value, place_of):
    pairs = []
    for row in range(ROWS):
        for col in range(COLS):
            to_row, to_col = place_of(row, col)
            pairs.append((COLS * row + col, COLS * to_row + to_col))
    with jax.named_scope(name):
        return lax.ppermute(value, ("row", "col"), pairs)


def after(value, *others):
    return lax.optimization_barrier((value, *others))[0]


def outward(value, name):
    return sent(name, value, lambda row, col: (row, col ^ 1))


def inward(value, name):
    return sent(name, value, lambda row, col: (row, 3 - col) if col in (1, 2) else (row ^ 1, col))


def second_over(value, name):
    return sent(name, value, lambda row, col: (row ^ 1, (2, 0, 3, 1)[col]) if col in (0, 3) else (row, (2, 0, 3, 1)[col]))


def end_to_end(value, name):
    return sent(name, value, lambda row, col: (row, 3 - col) if col in (0, 3) else (row ^ 1, col))


def swapped(value, name):
    return sent(name, value, lambda row, col: (row ^ 1, col))


def across(value, bits, name):
    return sent(name, value, lambda row, col: (row ^ bits, col))


def ax(value, name):
    return across(value, 2, name)


def ay(value, name):
    return across(value, 4, name)


def first_hop(value, name):
    return sent(name, value, lambda row, col: (row ^ (4 if row & 1 else 2), col))


def second_hop(value, name):
    return sent(name, value, lambda row, col: (row ^ (2 if row & 1 else 4), col))


def block_mesh(a_blocks, b_blocks, a_index, b_index, c_index, pair_count):
    row, col = lax.axis_index("row"), lax.axis_index("col")
    counts = pair_count[0, 0]
    packed = packed_lists(a_index[0, 0], b_index[0, 0], c_index[0, 0], counts)
    tables = stage_tables(a_index.shape[2])
    table = jnp.asarray(tables)[row, col].reshape(-1)
    a_own, b_own = a_blocks[0, 0], b_blocks[0, 0]
    def stage_call(stage, total):
        arrays, a_views, b_views = [], {}, {}

        def number_of(value):
            for number, held in enumerate(arrays):
                if held is value:
                    return number
            arrays.append(value)
            return len(arrays) - 1

        for place in used(tables, stage, 2):
            a_views[place] = tuple(number_of(value) for value in a_at[place])
        for source in used(tables, stage, 3):
            value, half = b_at[source]
            b_views[source] = (number_of(value), half)
        return run_stage(stage, table, counts, packed, arrays, a_views, b_views, total, stage == STAGES - 1, 150)

    O = outward(b_own, "O")
    I = inward(b_own, "I")
    H1 = first_hop(a_own, "H1")
    H2 = second_hop(a_own, "H2")
    W0 = swapped(a_own, "W0")
    S0 = outward(I[0], "S0")
    F0 = inward(after(O, packed, table)[0], "F0")
    S1 = outward(I[1], "S1")
    F1 = inward(O[1], "F1")
    Ha = second_hop(H1[:32], "Ha")
    Hb = second_hop(H1[32:], "Hb")
    W1 = swapped(H1, "W1")
    T0 = outward(F0, "T0")
    W3 = swapped(Ha, "W3")
    W4 = swapped(Hb, "W4")
    W2 = swapped(H2, "W2")
    T1 = outward(F1, "T1")
    a_at = [(a_own,), (W0,), (H1,), (W1,), (H2,), (W2,), (Ha, Hb), (W3, W4)]
    b_at = [(b_own, 0), (b_own, 1), (O, 0), (O, 1), (I, 0), (I, 1)]
    b_at += [(value, None) for value in (S0, S1, F0, F1, T0, T1)]
    total = None
    for stage in range(STAGES):
        total = stage_call(stage, total)
    return total[None, None]


def solution(mesh):
    placed = (
        P("row", "col", None, None, None),
        P("row", "col", None, None, None, None),
        P("row", "col", None, None),
        P("row", "col", None, None),
        P("row", "col", None, None),
        P("row", "col", None),
    )
    exact = (mesh.shape["row"], mesh.shape["col"]) == (ROWS, COLS)
    return jax.shard_map(
        block_mesh if exact else any_mesh,
        mesh=mesh,
        in_specs=placed,
        out_specs=P("row", "col", None, None, None),
        check_vma=False,
    )
```

```python
import functools

import jax
import jax.numpy as jnp
import numpy as np
from jax import lax
from jax.experimental import pallas as pl
from jax.experimental.pallas import tpu as pltpu
from jax.sharding import PartitionSpec as P

SLOTS_C = 64
GROUP = 32
BUFFERS = 3
FIELDS = 32
B_SHIFT, C_SHIFT = 8, 16
HBM = pl.BlockSpec(memory_space=pltpu.HBM)


def stage_kernel(table, counts, packed, *refs, stage, a_views, b_views, n_inputs, first, last):
    inputs = refs[:n_inputs]
    rest = refs[n_inputs:]
    c_in, rest = (None, rest) if first else (rest[0], rest[1:])
    out, total, a_buf, b_buf, b_turned, a_sem, b_sem, c_sem = rest[:8]
    rounded = rest[8] if last else None
    base = stage * FIELDS
    entries = table[base]
    slots_c = SLOTS_C

    def fetch(k, slot):
        a_id = table[base + 2 + 3 * k]
        b_id = table[base + 3 + 3 * k]
        for number, pieces in a_views.items():

            @pl.when(a_id == number)
            def _(pieces=pieces):
                size = a_buf.shape[1] // len(pieces)
                for piece, ref_number in enumerate(pieces):
                    target = a_buf.at[slot, pl.ds(piece * size, size)]
                    pltpu.make_async_copy(inputs[ref_number], target, a_sem.at[slot]).start()

        for number, (ref_number, half) in b_views.items():

            @pl.when(b_id == number)
            def _(ref_number=ref_number, half=half):
                source = inputs[ref_number] if half is None else inputs[ref_number].at[half]
                pltpu.make_async_copy(source, b_buf.at[slot], b_sem.at[slot]).start()

    def await_fetch(slot):
        pltpu.make_async_copy(a_buf.at[slot], a_buf.at[slot], a_sem.at[slot]).wait()
        pltpu.make_async_copy(b_buf.at[slot], b_buf.at[slot], b_sem.at[slot]).wait()

    if not first:
        brought = pltpu.make_async_copy(c_in, total.at[pl.ds(0, slots_c)], c_sem.at[0])
        brought.start()

    for ahead in range(BUFFERS - 1):

        @pl.when(ahead < entries)
        def _(ahead=ahead):
            fetch(ahead, ahead)

    if first:
        total[...] = jnp.zeros_like(total)
    else:
        total[pl.ds(slots_c, 1)] = jnp.zeros_like(total[pl.ds(slots_c, 1)])
        brought.wait()

    def one_tick(k, carry):
        slot = lax.rem(k, BUFFERS)
        await_fetch(slot)

        @pl.when(k + BUFFERS - 1 < entries)
        def _():
            fetch(k + BUFFERS - 1, lax.rem(k + BUFFERS - 1, BUFFERS))

        tick = table[base + 1 + 3 * k]
        for s in range(b_buf.shape[1]):
            b_turned[s] = b_buf[slot, s].T

        def one_group(g, carry):
            for u in range(GROUP):
                word = packed[tick, g * GROUP + u]
                a_at = word & 255
                b_at = (word >> B_SHIFT) & 255
                c_at = word >> C_SHIFT
                product = jnp.dot(a_buf[slot, a_at], b_turned[b_at], preferred_element_type=jnp.float32)
                total[c_at] = total[c_at] + product
            return carry

        lax.fori_loop(0, (counts[tick] + GROUP - 1) // GROUP, one_group, 0)
        return carry

    lax.fori_loop(0, entries, one_tick, 0)

    if last:
        chunk = 16
        copies = []
        for start in range(0, slots_c, chunk):
            part = pl.ds(start, chunk)
            rounded[part] = total[part].astype(jnp.bfloat16)
            copies.append(pltpu.make_async_copy(rounded.at[part], out.at[part], c_sem.at[start // chunk]))
            copies[-1].start()
        for copy in copies:
            copy.wait()
    else:
        done = pltpu.make_async_copy(total.at[pl.ds(0, slots_c)], out, c_sem.at[0])
        done.start()
        done.wait()


def run_stage(stage, table, counts, packed, arrays, a_views, b_views, c_in, last, pairs_hint):
    first = c_in is None
    slots_a = sum(arrays[number].shape[0] for number in next(iter(a_views.values())))
    slots_b, bs = arrays[next(iter(b_views.values()))[0]].shape[-3:-1]
    operands = list(arrays) + ([] if first else [c_in])
    kernel = functools.partial(
        stage_kernel,
        stage=stage,
        a_views=a_views,
        b_views=b_views,
        n_inputs=len(arrays),
        first=first,
        last=last,
    )
    scratch = [
        pltpu.VMEM((SLOTS_C + 1, bs, bs), jnp.float32),
        pltpu.VMEM((BUFFERS, slots_a, bs, bs), jnp.bfloat16),
        pltpu.VMEM((BUFFERS, slots_b, bs, bs), jnp.bfloat16),
        pltpu.VMEM((slots_b, bs, bs), jnp.bfloat16),
        pltpu.SemaphoreType.DMA((BUFFERS,)),
        pltpu.SemaphoreType.DMA((BUFFERS,)),
        pltpu.SemaphoreType.DMA((4,)),
    ]
    if last:
        scratch.append(pltpu.VMEM((SLOTS_C, bs, bs), jnp.bfloat16))
    return pl.pallas_call(
        kernel,
        out_shape=jax.ShapeDtypeStruct((SLOTS_C, bs, bs), jnp.bfloat16 if last else jnp.float32),
        grid_spec=pltpu.PrefetchScalarGridSpec(
            num_scalar_prefetch=3,
            grid=(1,),
            in_specs=[HBM] * len(operands),
            out_specs=HBM,
            scratch_shapes=scratch,
        ),
        compiler_params=pltpu.CompilerParams(vmem_limit_bytes=60 << 20),
        cost_estimate=pl.CostEstimate(
            flops=0, bytes_accessed=0, transcendentals=0
        ),
        name=f"stage{stage}",
    )(table, counts, packed, *operands)


def packed_lists(a_index, b_index, c_index, pair_count):
    position = lax.broadcasted_iota(jnp.int32, a_index.shape, 1)
    target = jnp.where(position < pair_count[:, None], c_index, SLOTS_C)
    return a_index | (b_index << B_SHIFT) | (target << C_SHIFT)


def shifted(value, axis, steps):
    count = lax.axis_size(axis)
    return lax.ppermute(value, axis, [(source, (source + steps) % count) for source in range(count)])


def any_mesh(a_blocks, b_blocks, a_index, b_index, c_index, pair_count):
    row, col = lax.axis_index("row"), lax.axis_index("col")
    rows, cols = lax.axis_size("row"), lax.axis_size("col")
    ticks = a_index.shape[2]
    back = ticks // 2 - 1
    counts = pair_count[0, 0]
    packed = packed_lists(a_index[0, 0], b_index[0, 0], c_index[0, 0], counts)
    a_now = shifted(a_blocks[0, 0], "row", back)
    b_now = shifted(b_blocks[0, 0], "col", back)
    halves = b_now.shape[0]
    running = None
    for tick in range(ticks):
        half = (row + col + tick - back) % rows // cols
        entry = jnp.concatenate(
            [jnp.array([1, tick, 0], jnp.int32), half[None].astype(jnp.int32), jnp.zeros((FIELDS - 4,), jnp.int32)]
        )
        running = run_stage(
            0, entry, counts, packed, [a_now, b_now],
            {0: (0,)}, {h: (1, h) for h in range(halves)},
            running, tick == ticks - 1, packed.shape[1],
        )
        if tick < ticks - 1:
            a_now = shifted(a_now, "row", -1)
            b_now = shifted(b_now, "col", -1)
    return running[None, None]


ROWS, COLS = 8, 4
OWN, OUTER, INNER, SECOND, INNER_FAR, THIRD = range(6)
A_STAGE = (0, 0, 0, 0, 0, 0, 0, 0)
B_STAGE = ((0, 0), (0, 0), (0, 0), (0, 0), (0, 0), (0, 1))
STAGES = 2


def a_place(row, target):
    delta = row ^ target
    by_core, hop = delta & 1, delta & 6
    if hop in (0, 6):
        return hop + by_core
    return (2 if (hop == 2) == ((row & 1) == by_core) else 4) + by_core


def b_source(col, target):
    if target == col:
        return OWN
    if col in (0, 3):
        return (None, OUTER, SECOND, THIRD)[abs(target - col)]
    if abs(target - col) == 2:
        return INNER_FAR
    return OUTER if target in (0, 3) else INNER


def stage_tables(ticks=8):
    tables = np.zeros((ROWS, COLS, STAGES, FIELDS), np.int32)
    for row in range(ROWS):
        for col in range(COLS):
            lists = [[] for _ in range(STAGES)]
            for tick in range(ticks):
                offset = tick - (ticks // 2 - 1)
                place = a_place(row, (row + offset) % ROWS)
                source = b_source(col, (col + offset) % COLS)
                half = (row + col + offset) % ROWS // COLS
                ready = max(A_STAGE[place], B_STAGE[source][half])
                lists[ready].append((tick, place, 2 * source + half))
            for stage, entries in enumerate(lists):
                tables[row, col, stage, 0] = len(entries)
                for k, entry in enumerate(entries):
                    tables[row, col, stage, 1 + 3 * k : 4 + 3 * k] = entry
    return tables


def used(tables, stage, field):
    found = set()
    for entries in tables[:, :, stage].reshape(-1, FIELDS):
        found |= {int(entries[field + 3 * k]) for k in range(entries[0])}
    return sorted(found)


def sent(name, value, place_of):
    pairs = []
    for row in range(ROWS):
        for col in range(COLS):
            to_row, to_col = place_of(row, col)
            pairs.append((COLS * row + col, COLS * to_row + to_col))
    with jax.named_scope(name):
        return lax.ppermute(value, ("row", "col"), pairs)


def after(value, *others):
    return lax.optimization_barrier((value, *others))[0]


def outward(value, name):
    return sent(name, value, lambda row, col: (row, col ^ 1))


def inward(value, name):
    return sent(name, value, lambda row, col: (row, 3 - col) if col in (1, 2) else (row ^ 1, col))


def second_over(value, name):
    return sent(name, value, lambda row, col: (row ^ 1, (2, 0, 3, 1)[col]) if col in (0, 3) else (row, (2, 0, 3, 1)[col]))


def end_to_end(value, name):
    return sent(name, value, lambda row, col: (row, 3 - col) if col in (0, 3) else (row ^ 1, col))


def swapped(value, name):
    return sent(name, value, lambda row, col: (row ^ 1, col))


def across(value, bits, name):
    return sent(name, value, lambda row, col: (row ^ bits, col))


def ax(value, name):
    return across(value, 2, name)


def ay(value, name):
    return across(value, 4, name)


def first_hop(value, name):
    return sent(name, value, lambda row, col: (row ^ (4 if row & 1 else 2), col))


def second_hop(value, name):
    return sent(name, value, lambda row, col: (row ^ (2 if row & 1 else 4), col))


def block_mesh(a_blocks, b_blocks, a_index, b_index, c_index, pair_count):
    row, col = lax.axis_index("row"), lax.axis_index("col")
    counts = pair_count[0, 0]
    packed = packed_lists(a_index[0, 0], b_index[0, 0], c_index[0, 0], counts)
    tables = stage_tables(a_index.shape[2])
    table = jnp.asarray(tables)[row, col].reshape(-1)
    a_own, b_own = a_blocks[0, 0], b_blocks[0, 0]
    def stage_call(stage, total):
        arrays, a_views, b_views = [], {}, {}

        def number_of(value):
            for number, held in enumerate(arrays):
                if held is value:
                    return number
            arrays.append(value)
            return len(arrays) - 1

        for place in used(tables, stage, 2):
            a_views[place] = tuple(number_of(value) for value in a_at[place])
        for source in used(tables, stage, 3):
            value, half = b_at[source]
            b_views[source] = (number_of(value), half)
        return run_stage(stage, table, counts, packed, arrays, a_views, b_views, total, stage == STAGES - 1, 150)

    O = outward(b_own, "O")
    I = inward(b_own, "I")
    H1 = first_hop(a_own, "H1")
    H2 = second_hop(a_own, "H2")
    W0 = swapped(a_own, "W0")
    S0 = outward(I[0], "S0")
    F0 = inward(after(O, W0, packed, table)[0], "F0")
    S1 = outward(I[1], "S1")
    F1 = inward(O[1], "F1")
    Ha = second_hop(H1[:32], "Ha")
    Hb = second_hop(H1[32:], "Hb")
    W1 = swapped(after(H1, S1), "W1")
    T0 = outward(F0, "T0")
    W3 = swapped(Ha, "W3")
    W4 = swapped(Hb, "W4")
    W2 = swapped(after(H2, S1), "W2")
    T1 = outward(F1, "T1")
    a_at = [(a_own,), (W0,), (H1,), (W1,), (H2,), (W2,), (Ha, Hb), (W3, W4)]
    b_at = [(b_own, 0), (b_own, 1), (O, 0), (O, 1), (I, 0), (I, 1)]
    b_at += [(value, None) for value in (S0, S1, F0, F1, T0, T1)]
    total = None
    for stage in range(STAGES):
        total = stage_call(stage, total)
    return total[None, None]


def solution(mesh):
    placed = (
        P("row", "col", None, None, None),
        P("row", "col", None, None, None, None),
        P("row", "col", None, None),
        P("row", "col", None, None),
        P("row", "col", None, None),
        P("row", "col", None),
    )
    exact = (mesh.shape["row"], mesh.shape["col"]) == (ROWS, COLS)
    return jax.shard_map(
        block_mesh if exact else any_mesh,
        mesh=mesh,
        in_specs=placed,
        out_specs=P("row", "col", None, None, None),
        check_vma=False,
    )
```

```python
import functools

import jax
import jax.numpy as jnp
import numpy as np
from jax import lax
from jax.experimental import pallas as pl
from jax.experimental.pallas import tpu as pltpu
from jax.sharding import PartitionSpec as P

SLOTS_C = 64
GROUP = 32
BUFFERS = 3
FIELDS = 32
B_SHIFT, C_SHIFT = 8, 16
HBM = pl.BlockSpec(memory_space=pltpu.HBM)


def stage_kernel(table, counts, packed, *refs, stage, a_views, b_views, n_inputs, first, last):
    inputs = refs[:n_inputs]
    rest = refs[n_inputs:]
    c_in, rest = (None, rest) if first else (rest[0], rest[1:])
    out, total, a_buf, b_buf, b_turned, a_sem, b_sem, c_sem = rest[:8]
    before = None if first else rest[8]
    rounded = rest[-1] if last else None
    base = stage * FIELDS
    entries = table[base]
    slots_c = SLOTS_C

    def fetch(k, slot):
        a_id = table[base + 2 + 3 * k]
        b_id = table[base + 3 + 3 * k]
        for number, pieces in a_views.items():

            @pl.when(a_id == number)
            def _(pieces=pieces):
                size = a_buf.shape[1] // len(pieces)
                for piece, ref_number in enumerate(pieces):
                    target = a_buf.at[slot, pl.ds(piece * size, size)]
                    pltpu.make_async_copy(inputs[ref_number], target, a_sem.at[slot]).start()

        for number, (ref_number, half) in b_views.items():

            @pl.when(b_id == number)
            def _(ref_number=ref_number, half=half):
                source = inputs[ref_number] if half is None else inputs[ref_number].at[half]
                pltpu.make_async_copy(source, b_buf.at[slot], b_sem.at[slot]).start()

    def await_fetch(slot):
        pltpu.make_async_copy(a_buf.at[slot], a_buf.at[slot], a_sem.at[slot]).wait()
        pltpu.make_async_copy(b_buf.at[slot], b_buf.at[slot], b_sem.at[slot]).wait()

    for ahead in range(BUFFERS - 1):

        @pl.when(ahead < entries)
        def _(ahead=ahead):
            fetch(ahead, ahead)

    total[...] = jnp.zeros_like(total)
    if not first:
        brought = pltpu.make_async_copy(c_in, before, c_sem.at[0])
        brought.start()

    def one_tick(k, carry):
        slot = lax.rem(k, BUFFERS)
        await_fetch(slot)

        @pl.when(k + BUFFERS - 1 < entries)
        def _():
            fetch(k + BUFFERS - 1, lax.rem(k + BUFFERS - 1, BUFFERS))

        tick = table[base + 1 + 3 * k]
        for s in range(b_buf.shape[1]):
            b_turned[s] = b_buf[slot, s].T

        def one_group(g, carry):
            for u in range(GROUP):
                word = packed[tick, g * GROUP + u]
                a_at = word & 255
                b_at = (word >> B_SHIFT) & 255
                c_at = word >> C_SHIFT
                product = jnp.dot(a_buf[slot, a_at], b_turned[b_at], preferred_element_type=jnp.float32)
                total[c_at] = total[c_at] + product
            return carry

        lax.fori_loop(0, (counts[tick] + GROUP - 1) // GROUP, one_group, 0)
        return carry

    lax.fori_loop(0, entries, one_tick, 0)

    if not first:
        brought.wait()
    if last:
        chunk = 8
        copies = []
        for start in range(0, slots_c, chunk):
            part = pl.ds(start, chunk)
            summed = total[part] if first else total[part] + before[part]
            rounded[part] = summed.astype(jnp.bfloat16)
            copies.append(pltpu.make_async_copy(rounded.at[part], out.at[part], c_sem.at[start // chunk]))
            copies[-1].start()
        for copy in copies:
            copy.wait()
    else:
        if not first:
            total[pl.ds(0, slots_c)] = total[pl.ds(0, slots_c)] + before[...]
        done = pltpu.make_async_copy(total.at[pl.ds(0, slots_c)], out, c_sem.at[0])
        done.start()
        done.wait()


def run_stage(stage, table, counts, packed, arrays, a_views, b_views, c_in, last, pairs_hint):
    first = c_in is None
    slots_a = sum(arrays[number].shape[0] for number in next(iter(a_views.values())))
    slots_b, bs = arrays[next(iter(b_views.values()))[0]].shape[-3:-1]
    operands = list(arrays) + ([] if first else [c_in])
    kernel = functools.partial(
        stage_kernel,
        stage=stage,
        a_views=a_views,
        b_views=b_views,
        n_inputs=len(arrays),
        first=first,
        last=last,
    )
    scratch = [
        pltpu.VMEM((SLOTS_C + 1, bs, bs), jnp.float32),
        pltpu.VMEM((BUFFERS, slots_a, bs, bs), jnp.bfloat16),
        pltpu.VMEM((BUFFERS, slots_b, bs, bs), jnp.bfloat16),
        pltpu.VMEM((slots_b, bs, bs), jnp.bfloat16),
        pltpu.SemaphoreType.DMA((BUFFERS,)),
        pltpu.SemaphoreType.DMA((BUFFERS,)),
        pltpu.SemaphoreType.DMA((8,)),
    ]
    if not first:
        scratch.append(pltpu.VMEM((SLOTS_C, bs, bs), jnp.float32))
    if last:
        scratch.append(pltpu.VMEM((SLOTS_C, bs, bs), jnp.bfloat16))
    return pl.pallas_call(
        kernel,
        out_shape=jax.ShapeDtypeStruct((SLOTS_C, bs, bs), jnp.bfloat16 if last else jnp.float32),
        grid_spec=pltpu.PrefetchScalarGridSpec(
            num_scalar_prefetch=3,
            grid=(1,),
            in_specs=[HBM] * len(operands),
            out_specs=HBM,
            scratch_shapes=scratch,
        ),
        compiler_params=pltpu.CompilerParams(vmem_limit_bytes=60 << 20),
        cost_estimate=pl.CostEstimate(
            flops=0, bytes_accessed=0, transcendentals=0
        ),
        name=f"stage{stage}",
    )(table, counts, packed, *operands)


def packed_lists(a_index, b_index, c_index, pair_count):
    position = lax.broadcasted_iota(jnp.int32, a_index.shape, 1)
    target = jnp.where(position < pair_count[:, None], c_index, SLOTS_C)
    return a_index | (b_index << B_SHIFT) | (target << C_SHIFT)


def shifted(value, axis, steps):
    count = lax.axis_size(axis)
    return lax.ppermute(value, axis, [(source, (source + steps) % count) for source in range(count)])


def any_mesh(a_blocks, b_blocks, a_index, b_index, c_index, pair_count):
    row, col = lax.axis_index("row"), lax.axis_index("col")
    rows, cols = lax.axis_size("row"), lax.axis_size("col")
    ticks = a_index.shape[2]
    back = ticks // 2 - 1
    counts = pair_count[0, 0]
    packed = packed_lists(a_index[0, 0], b_index[0, 0], c_index[0, 0], counts)
    a_now = shifted(a_blocks[0, 0], "row", back)
    b_now = shifted(b_blocks[0, 0], "col", back)
    halves = b_now.shape[0]
    running = None
    for tick in range(ticks):
        half = (row + col + tick - back) % rows // cols
        entry = jnp.concatenate(
            [jnp.array([1, tick, 0], jnp.int32), half[None].astype(jnp.int32), jnp.zeros((FIELDS - 4,), jnp.int32)]
        )
        running = run_stage(
            0, entry, counts, packed, [a_now, b_now],
            {0: (0,)}, {h: (1, h) for h in range(halves)},
            running, tick == ticks - 1, packed.shape[1],
        )
        if tick < ticks - 1:
            a_now = shifted(a_now, "row", -1)
            b_now = shifted(b_now, "col", -1)
    return running[None, None]


ROWS, COLS = 8, 4
OWN, OUTER, INNER, SECOND, INNER_FAR, THIRD = range(6)
A_STAGE = (0, 0, 0, 0, 0, 0, 0, 0)
B_STAGE = ((0, 0), (0, 0), (0, 0), (0, 0), (0, 0), (0, 1))
STAGES = 2


def a_place(row, target):
    delta = row ^ target
    by_core, hop = delta & 1, delta & 6
    if hop in (0, 6):
        return hop + by_core
    return (2 if (hop == 2) == ((row & 1) == by_core) else 4) + by_core


def b_source(col, target):
    if target == col:
        return OWN
    if col in (0, 3):
        return (None, OUTER, SECOND, THIRD)[abs(target - col)]
    if abs(target - col) == 2:
        return INNER_FAR
    return OUTER if target in (0, 3) else INNER


def stage_tables(ticks=8):
    tables = np.zeros((ROWS, COLS, STAGES, FIELDS), np.int32)
    for row in range(ROWS):
        for col in range(COLS):
            lists = [[] for _ in range(STAGES)]
            for tick in range(ticks):
                offset = tick - (ticks // 2 - 1)
                place = a_place(row, (row + offset) % ROWS)
                source = b_source(col, (col + offset) % COLS)
                half = (row + col + offset) % ROWS // COLS
                ready = max(A_STAGE[place], B_STAGE[source][half])
                lists[ready].append((tick, place, 2 * source + half))
            for stage, entries in enumerate(lists):
                tables[row, col, stage, 0] = len(entries)
                for k, entry in enumerate(entries):
                    tables[row, col, stage, 1 + 3 * k : 4 + 3 * k] = entry
    return tables


def used(tables, stage, field):
    found = set()
    for entries in tables[:, :, stage].reshape(-1, FIELDS):
        found |= {int(entries[field + 3 * k]) for k in range(entries[0])}
    return sorted(found)


def sent(name, value, place_of):
    pairs = []
    for row in range(ROWS):
        for col in range(COLS):
            to_row, to_col = place_of(row, col)
            pairs.append((COLS * row + col, COLS * to_row + to_col))
    with jax.named_scope(name):
        return lax.ppermute(value, ("row", "col"), pairs)


def after(value, *others):
    return lax.optimization_barrier((value, *others))[0]


def outward(value, name):
    return sent(name, value, lambda row, col: (row, col ^ 1))


def inward(value, name):
    return sent(name, value, lambda row, col: (row, 3 - col) if col in (1, 2) else (row ^ 1, col))


def second_over(value, name):
    return sent(name, value, lambda row, col: (row ^ 1, (2, 0, 3, 1)[col]) if col in (0, 3) else (row, (2, 0, 3, 1)[col]))


def end_to_end(value, name):
    return sent(name, value, lambda row, col: (row, 3 - col) if col in (0, 3) else (row ^ 1, col))


def swapped(value, name):
    return sent(name, value, lambda row, col: (row ^ 1, col))


def across(value, bits, name):
    return sent(name, value, lambda row, col: (row ^ bits, col))


def ax(value, name):
    return across(value, 2, name)


def ay(value, name):
    return across(value, 4, name)


def first_hop(value, name):
    return sent(name, value, lambda row, col: (row ^ (4 if row & 1 else 2), col))


def second_hop(value, name):
    return sent(name, value, lambda row, col: (row ^ (2 if row & 1 else 4), col))


def block_mesh(a_blocks, b_blocks, a_index, b_index, c_index, pair_count):
    row, col = lax.axis_index("row"), lax.axis_index("col")
    counts = pair_count[0, 0]
    packed = packed_lists(a_index[0, 0], b_index[0, 0], c_index[0, 0], counts)
    tables = stage_tables(a_index.shape[2])
    table = jnp.asarray(tables)[row, col].reshape(-1)
    a_own, b_own = a_blocks[0, 0], b_blocks[0, 0]
    def stage_call(stage, total):
        arrays, a_views, b_views = [], {}, {}

        def number_of(value):
            for number, held in enumerate(arrays):
                if held is value:
                    return number
            arrays.append(value)
            return len(arrays) - 1

        for place in used(tables, stage, 2):
            a_views[place] = tuple(number_of(value) for value in a_at[place])
        for source in used(tables, stage, 3):
            value, half = b_at[source]
            b_views[source] = (number_of(value), half)
        return run_stage(stage, table, counts, packed, arrays, a_views, b_views, total, stage == STAGES - 1, 150)

    O = outward(b_own, "O")
    I = inward(b_own, "I")
    H1 = first_hop(a_own, "H1")
    H2 = second_hop(a_own, "H2")
    W0 = swapped(a_own, "W0")
    S0 = outward(I[0], "S0")
    F0 = inward(after(O, W0, packed, table)[0], "F0")
    S1 = outward(I[1], "S1")
    F1 = inward(O[1], "F1")
    Ha = second_hop(H1[:32], "Ha")
    Hb = second_hop(H1[32:], "Hb")
    W1 = swapped(after(H1, S1), "W1")
    T0 = outward(F0, "T0")
    W3 = swapped(Ha, "W3")
    W4 = swapped(Hb, "W4")
    W2 = swapped(after(H2, S1), "W2")
    T1 = outward(after(F1, S0), "T1")
    a_at = [(a_own,), (W0,), (H1,), (W1,), (H2,), (W2,), (Ha, Hb), (W3, W4)]
    b_at = [(b_own, 0), (b_own, 1), (O, 0), (O, 1), (I, 0), (I, 1)]
    b_at += [(value, None) for value in (S0, S1, F0, F1, T0, T1)]
    total = None
    for stage in range(STAGES):
        total = stage_call(stage, total)
    return total[None, None]


def solution(mesh):
    placed = (
        P("row", "col", None, None, None),
        P("row", "col", None, None, None, None),
        P("row", "col", None, None),
        P("row", "col", None, None),
        P("row", "col", None, None),
        P("row", "col", None),
    )
    exact = (mesh.shape["row"], mesh.shape["col"]) == (ROWS, COLS)
    return jax.shard_map(
        block_mesh if exact else any_mesh,
        mesh=mesh,
        in_specs=placed,
        out_specs=P("row", "col", None, None, None),
        check_vma=False,
    )
```

```python
import functools

import jax
import jax.numpy as jnp
import numpy as np
from jax import lax
from jax.experimental import pallas as pl
from jax.experimental.pallas import tpu as pltpu
from jax.sharding import PartitionSpec as P

SLOTS_C = 64
GROUP = 32
BUFFERS = 5
FIELDS = 32
B_SHIFT, C_SHIFT = 8, 16
HBM = pl.BlockSpec(memory_space=pltpu.HBM)


def stage_kernel(table, counts, packed, *refs, stage, a_views, b_views, n_inputs, first, last):
    inputs = refs[:n_inputs]
    rest = refs[n_inputs:]
    c_in, rest = (None, rest) if first else (rest[0], rest[1:])
    out, total, a_buf, b_buf, b_turned, a_sem, b_sem, c_sem = rest[:8]
    before = None if first else rest[8]
    rounded = rest[-1] if last else None
    base = stage * FIELDS
    entries = table[base]
    slots_c = SLOTS_C

    def fetch(k, slot):
        a_id = table[base + 2 + 3 * k]
        b_id = table[base + 3 + 3 * k]
        for number, pieces in a_views.items():

            @pl.when(a_id == number)
            def _(pieces=pieces):
                size = a_buf.shape[1] // len(pieces)
                for piece, ref_number in enumerate(pieces):
                    target = a_buf.at[slot, pl.ds(piece * size, size)]
                    pltpu.make_async_copy(inputs[ref_number], target, a_sem.at[slot]).start()

        for number, (ref_number, half) in b_views.items():

            @pl.when(b_id == number)
            def _(ref_number=ref_number, half=half):
                source = inputs[ref_number] if half is None else inputs[ref_number].at[half]
                pltpu.make_async_copy(source, b_buf.at[slot], b_sem.at[slot]).start()

    def await_fetch(slot):
        pltpu.make_async_copy(a_buf.at[slot], a_buf.at[slot], a_sem.at[slot]).wait()
        pltpu.make_async_copy(b_buf.at[slot], b_buf.at[slot], b_sem.at[slot]).wait()

    for ahead in range(BUFFERS - 1):

        @pl.when(ahead < entries)
        def _(ahead=ahead):
            fetch(ahead, ahead)

    total[...] = jnp.zeros_like(total)
    if not first:
        brought = pltpu.make_async_copy(c_in, before, c_sem.at[0])
        brought.start()

    def one_tick(k, carry):
        slot = lax.rem(k, BUFFERS)
        await_fetch(slot)

        @pl.when(k + BUFFERS - 1 < entries)
        def _():
            fetch(k + BUFFERS - 1, lax.rem(k + BUFFERS - 1, BUFFERS))

        tick = table[base + 1 + 3 * k]
        for s in range(b_buf.shape[1]):
            b_turned[s] = b_buf[slot, s].T

        def one_group(g, carry):
            for u in range(GROUP):
                word = packed[tick, g * GROUP + u]
                a_at = word & 255
                b_at = (word >> B_SHIFT) & 255
                c_at = word >> C_SHIFT
                product = jnp.dot(a_buf[slot, a_at], b_turned[b_at], preferred_element_type=jnp.float32)
                total[c_at] = total[c_at] + product
            return carry

        lax.fori_loop(0, (counts[tick] + GROUP - 1) // GROUP, one_group, 0)
        return carry

    lax.fori_loop(0, entries, one_tick, 0)

    if not first:
        brought.wait()
    if last:
        chunk = 8
        copies = []
        for start in range(0, slots_c, chunk):
            part = pl.ds(start, chunk)
            summed = total[part] if first else total[part] + before[part]
            rounded[part] = summed.astype(jnp.bfloat16)
            copies.append(pltpu.make_async_copy(rounded.at[part], out.at[part], c_sem.at[start // chunk]))
            copies[-1].start()
        for copy in copies:
            copy.wait()
    else:
        if not first:
            total[pl.ds(0, slots_c)] = total[pl.ds(0, slots_c)] + before[...]
        done = pltpu.make_async_copy(total.at[pl.ds(0, slots_c)], out, c_sem.at[0])
        done.start()
        done.wait()


def run_stage(stage, table, counts, packed, arrays, a_views, b_views, c_in, last, pairs_hint):
    first = c_in is None
    slots_a = sum(arrays[number].shape[0] for number in next(iter(a_views.values())))
    slots_b, bs = arrays[next(iter(b_views.values()))[0]].shape[-3:-1]
    operands = list(arrays) + ([] if first else [c_in])
    kernel = functools.partial(
        stage_kernel,
        stage=stage,
        a_views=a_views,
        b_views=b_views,
        n_inputs=len(arrays),
        first=first,
        last=last,
    )
    scratch = [
        pltpu.VMEM((SLOTS_C + 1, bs, bs), jnp.float32),
        pltpu.VMEM((BUFFERS, slots_a, bs, bs), jnp.bfloat16),
        pltpu.VMEM((BUFFERS, slots_b, bs, bs), jnp.bfloat16),
        pltpu.VMEM((slots_b, bs, bs), jnp.bfloat16),
        pltpu.SemaphoreType.DMA((BUFFERS,)),
        pltpu.SemaphoreType.DMA((BUFFERS,)),
        pltpu.SemaphoreType.DMA((8,)),
    ]
    if not first:
        scratch.append(pltpu.VMEM((SLOTS_C, bs, bs), jnp.float32))
    if last:
        scratch.append(pltpu.VMEM((SLOTS_C, bs, bs), jnp.bfloat16))
    return pl.pallas_call(
        kernel,
        out_shape=jax.ShapeDtypeStruct((SLOTS_C, bs, bs), jnp.bfloat16 if last else jnp.float32),
        grid_spec=pltpu.PrefetchScalarGridSpec(
            num_scalar_prefetch=3,
            grid=(1,),
            in_specs=[HBM] * len(operands),
            out_specs=HBM,
            scratch_shapes=scratch,
        ),
        compiler_params=pltpu.CompilerParams(vmem_limit_bytes=60 << 20),
        cost_estimate=pl.CostEstimate(
            flops=0, bytes_accessed=0, transcendentals=0
        ),
        name=f"stage{stage}",
    )(table, counts, packed, *operands)


def packed_lists(a_index, b_index, c_index, pair_count):
    position = lax.broadcasted_iota(jnp.int32, a_index.shape, 1)
    target = jnp.where(position < pair_count[:, None], c_index, SLOTS_C)
    return a_index | (b_index << B_SHIFT) | (target << C_SHIFT)


def shifted(value, axis, steps):
    count = lax.axis_size(axis)
    return lax.ppermute(value, axis, [(source, (source + steps) % count) for source in range(count)])


def any_mesh(a_blocks, b_blocks, a_index, b_index, c_index, pair_count):
    row, col = lax.axis_index("row"), lax.axis_index("col")
    rows, cols = lax.axis_size("row"), lax.axis_size("col")
    ticks = a_index.shape[2]
    back = ticks // 2 - 1
    counts = pair_count[0, 0]
    packed = packed_lists(a_index[0, 0], b_index[0, 0], c_index[0, 0], counts)
    a_now = shifted(a_blocks[0, 0], "row", back)
    b_now = shifted(b_blocks[0, 0], "col", back)
    halves = b_now.shape[0]
    running = None
    for tick in range(ticks):
        half = (row + col + tick - back) % rows // cols
        entry = jnp.concatenate(
            [jnp.array([1, tick, 0], jnp.int32), half[None].astype(jnp.int32), jnp.zeros((FIELDS - 4,), jnp.int32)]
        )
        running = run_stage(
            0, entry, counts, packed, [a_now, b_now],
            {0: (0,)}, {h: (1, h) for h in range(halves)},
            running, tick == ticks - 1, packed.shape[1],
        )
        if tick < ticks - 1:
            a_now = shifted(a_now, "row", -1)
            b_now = shifted(b_now, "col", -1)
    return running[None, None]


ROWS, COLS = 8, 4
OWN, OUTER, INNER, SECOND, INNER_FAR, THIRD = range(6)
A_STAGE = (0, 0, 0, 0, 0, 0, 0, 0)
B_STAGE = ((0, 0), (0, 0), (0, 0), (0, 0), (0, 0), (0, 1))
STAGES = 2


def a_place(row, target):
    delta = row ^ target
    by_core, hop = delta & 1, delta & 6
    if hop in (0, 6):
        return hop + by_core
    return (2 if (hop == 2) == ((row & 1) == by_core) else 4) + by_core


def b_source(col, target):
    if target == col:
        return OWN
    if col in (0, 3):
        return (None, OUTER, SECOND, THIRD)[abs(target - col)]
    if abs(target - col) == 2:
        return INNER_FAR
    return OUTER if target in (0, 3) else INNER


def stage_tables(ticks=8):
    tables = np.zeros((ROWS, COLS, STAGES, FIELDS), np.int32)
    for row in range(ROWS):
        for col in range(COLS):
            lists = [[] for _ in range(STAGES)]
            for tick in range(ticks):
                offset = tick - (ticks // 2 - 1)
                place = a_place(row, (row + offset) % ROWS)
                source = b_source(col, (col + offset) % COLS)
                half = (row + col + offset) % ROWS // COLS
                ready = max(A_STAGE[place], B_STAGE[source][half])
                lists[ready].append((tick, place, 2 * source + half))
            for stage, entries in enumerate(lists):
                tables[row, col, stage, 0] = len(entries)
                for k, entry in enumerate(entries):
                    tables[row, col, stage, 1 + 3 * k : 4 + 3 * k] = entry
    return tables


def used(tables, stage, field):
    found = set()
    for entries in tables[:, :, stage].reshape(-1, FIELDS):
        found |= {int(entries[field + 3 * k]) for k in range(entries[0])}
    return sorted(found)


def sent(name, value, place_of):
    pairs = []
    for row in range(ROWS):
        for col in range(COLS):
            to_row, to_col = place_of(row, col)
            pairs.append((COLS * row + col, COLS * to_row + to_col))
    with jax.named_scope(name):
        return lax.ppermute(value, ("row", "col"), pairs)


def after(value, *others):
    return lax.optimization_barrier((value, *others))[0]


def outward(value, name):
    return sent(name, value, lambda row, col: (row, col ^ 1))


def inward(value, name):
    return sent(name, value, lambda row, col: (row, 3 - col) if col in (1, 2) else (row ^ 1, col))


def second_over(value, name):
    return sent(name, value, lambda row, col: (row ^ 1, (2, 0, 3, 1)[col]) if col in (0, 3) else (row, (2, 0, 3, 1)[col]))


def end_to_end(value, name):
    return sent(name, value, lambda row, col: (row, 3 - col) if col in (0, 3) else (row ^ 1, col))


def swapped(value, name):
    return sent(name, value, lambda row, col: (row ^ 1, col))


def across(value, bits, name):
    return sent(name, value, lambda row, col: (row ^ bits, col))


def ax(value, name):
    return across(value, 2, name)


def ay(value, name):
    return across(value, 4, name)


def first_hop(value, name):
    return sent(name, value, lambda row, col: (row ^ (4 if row & 1 else 2), col))


def second_hop(value, name):
    return sent(name, value, lambda row, col: (row ^ (2 if row & 1 else 4), col))


def block_mesh(a_blocks, b_blocks, a_index, b_index, c_index, pair_count):
    row, col = lax.axis_index("row"), lax.axis_index("col")
    counts = pair_count[0, 0]
    packed = packed_lists(a_index[0, 0], b_index[0, 0], c_index[0, 0], counts)
    tables = stage_tables(a_index.shape[2])
    table = jnp.asarray(tables)[row, col].reshape(-1)
    a_own, b_own = a_blocks[0, 0], b_blocks[0, 0]
    def stage_call(stage, total):
        arrays, a_views, b_views = [], {}, {}

        def number_of(value):
            for number, held in enumerate(arrays):
                if held is value:
                    return number
            arrays.append(value)
            return len(arrays) - 1

        for place in used(tables, stage, 2):
            a_views[place] = tuple(number_of(value) for value in a_at[place])
        for source in used(tables, stage, 3):
            value, half = b_at[source]
            b_views[source] = (number_of(value), half)
        return run_stage(stage, table, counts, packed, arrays, a_views, b_views, total, stage == STAGES - 1, 150)

    O = outward(b_own, "O")
    I = inward(b_own, "I")
    H1 = first_hop(a_own, "H1")
    H2 = second_hop(a_own, "H2")
    W0 = swapped(a_own, "W0")
    S0 = outward(I[0], "S0")
    F0 = inward(after(O, W0, packed, table)[0], "F0")
    S1 = outward(I[1], "S1")
    F1 = inward(O[1], "F1")
    Ha = second_hop(H1[:32], "Ha")
    Hb = second_hop(H1[32:], "Hb")
    W1 = swapped(after(H1, S1), "W1")
    T0 = outward(F0, "T0")
    W3 = swapped(Ha, "W3")
    W4 = swapped(Hb, "W4")
    W2 = swapped(after(H2, S1), "W2")
    T1 = outward(after(F1, S0), "T1")
    a_at = [(a_own,), (W0,), (H1,), (W1,), (H2,), (W2,), (Ha, Hb), (W3, W4)]
    b_at = [(b_own, 0), (b_own, 1), (O, 0), (O, 1), (I, 0), (I, 1)]
    b_at += [(value, None) for value in (S0, S1, F0, F1, T0, T1)]
    total = None
    for stage in range(STAGES):
        total = stage_call(stage, total)
    return total[None, None]


def solution(mesh):
    placed = (
        P("row", "col", None, None, None),
        P("row", "col", None, None, None, None),
        P("row", "col", None, None),
        P("row", "col", None, None),
        P("row", "col", None, None),
        P("row", "col", None),
    )
    exact = (mesh.shape["row"], mesh.shape["col"]) == (ROWS, COLS)
    return jax.shard_map(
        block_mesh if exact else any_mesh,
        mesh=mesh,
        in_specs=placed,
        out_specs=P("row", "col", None, None, None),
        check_vma=False,
    )
```

```python
import functools

import jax
import jax.numpy as jnp
import numpy as np
from jax import lax
from jax.experimental import pallas as pl
from jax.experimental.pallas import tpu as pltpu
from jax.sharding import PartitionSpec as P

SLOTS_C = 64
GROUP = 32
BUFFERS = 5
FIELDS = 32
B_SHIFT, C_SHIFT = 8, 16
HBM = pl.BlockSpec(memory_space=pltpu.HBM)


def stage_kernel(table, counts, packed, *refs, stage, a_views, b_views, n_inputs, first, last):
    inputs = refs[:n_inputs]
    rest = refs[n_inputs:]
    c_in, rest = (None, rest) if first else (rest[0], rest[1:])
    out, total, a_buf, b_buf, b_turned, a_sem, b_sem, c_sem = rest[:8]
    before = None if first else rest[8]
    rounded = rest[-1] if last else None
    base = stage * FIELDS
    entries = table[base]
    slots_c = SLOTS_C

    def fetch(k, slot):
        a_id = table[base + 2 + 3 * k]
        b_id = table[base + 3 + 3 * k]
        for number, pieces in a_views.items():

            @pl.when(a_id == number)
            def _(pieces=pieces):
                size = a_buf.shape[1] // len(pieces)
                for piece, ref_number in enumerate(pieces):
                    target = a_buf.at[slot, pl.ds(piece * size, size)]
                    pltpu.make_async_copy(inputs[ref_number], target, a_sem.at[slot]).start()

        for number, (ref_number, half) in b_views.items():

            @pl.when(b_id == number)
            def _(ref_number=ref_number, half=half):
                source = inputs[ref_number] if half is None else inputs[ref_number].at[half]
                pltpu.make_async_copy(source, b_buf.at[slot], b_sem.at[slot]).start()

    def await_fetch(slot):
        pltpu.make_async_copy(a_buf.at[slot], a_buf.at[slot], a_sem.at[slot]).wait()
        pltpu.make_async_copy(b_buf.at[slot], b_buf.at[slot], b_sem.at[slot]).wait()

    for ahead in range(BUFFERS - 1):

        @pl.when(ahead < entries)
        def _(ahead=ahead):
            fetch(ahead, ahead)

    total[...] = jnp.zeros_like(total)
    if not first:
        brought = pltpu.make_async_copy(c_in, before, c_sem.at[0])
        brought.start()

    def one_tick(k, carry):
        slot = lax.rem(k, BUFFERS)
        await_fetch(slot)

        @pl.when(k + BUFFERS - 1 < entries)
        def _():
            fetch(k + BUFFERS - 1, lax.rem(k + BUFFERS - 1, BUFFERS))

        tick = table[base + 1 + 3 * k]
        for s in range(b_buf.shape[1]):
            b_turned[s] = b_buf[slot, s].T

        def one_group(g, carry):
            for u in range(GROUP):
                word = packed[tick, g * GROUP + u]
                a_at = word & 255
                b_at = (word >> B_SHIFT) & 255
                c_at = word >> C_SHIFT
                product = jnp.dot(a_buf[slot, a_at], b_turned[b_at], preferred_element_type=jnp.float32)
                total[c_at] = total[c_at] + product
            return carry

        lax.fori_loop(0, (counts[tick] + GROUP - 1) // GROUP, one_group, 0)
        return carry

    lax.fori_loop(0, entries, one_tick, 0)

    if not first:
        brought.wait()
    if last:
        chunk = 8
        copies = []
        for start in range(0, slots_c, chunk):
            part = pl.ds(start, chunk)
            summed = total[part] if first else total[part] + before[part]
            rounded[part] = summed.astype(jnp.bfloat16)
            copies.append(pltpu.make_async_copy(rounded.at[part], out.at[part], c_sem.at[start // chunk]))
            copies[-1].start()
        for copy in copies:
            copy.wait()
    else:
        if not first:
            total[pl.ds(0, slots_c)] = total[pl.ds(0, slots_c)] + before[...]
        done = pltpu.make_async_copy(total.at[pl.ds(0, slots_c)], out, c_sem.at[0])
        done.start()
        done.wait()


def run_stage(stage, table, counts, packed, arrays, a_views, b_views, c_in, last, pairs_hint):
    first = c_in is None
    slots_a = sum(arrays[number].shape[0] for number in next(iter(a_views.values())))
    slots_b, bs = arrays[next(iter(b_views.values()))[0]].shape[-3:-1]
    operands = list(arrays) + ([] if first else [c_in])
    kernel = functools.partial(
        stage_kernel,
        stage=stage,
        a_views=a_views,
        b_views=b_views,
        n_inputs=len(arrays),
        first=first,
        last=last,
    )
    scratch = [
        pltpu.VMEM((SLOTS_C + 1, bs, bs), jnp.float32),
        pltpu.VMEM((BUFFERS, slots_a, bs, bs), jnp.bfloat16),
        pltpu.VMEM((BUFFERS, slots_b, bs, bs), jnp.bfloat16),
        pltpu.VMEM((slots_b, bs, bs), jnp.bfloat16),
        pltpu.SemaphoreType.DMA((BUFFERS,)),
        pltpu.SemaphoreType.DMA((BUFFERS,)),
        pltpu.SemaphoreType.DMA((8,)),
    ]
    if not first:
        scratch.append(pltpu.VMEM((SLOTS_C, bs, bs), jnp.float32))
    if last:
        scratch.append(pltpu.VMEM((SLOTS_C, bs, bs), jnp.bfloat16))
    return pl.pallas_call(
        kernel,
        out_shape=jax.ShapeDtypeStruct((SLOTS_C, bs, bs), jnp.bfloat16 if last else jnp.float32),
        grid_spec=pltpu.PrefetchScalarGridSpec(
            num_scalar_prefetch=3,
            grid=(1,),
            in_specs=[HBM] * len(operands),
            out_specs=HBM,
            scratch_shapes=scratch,
        ),
        compiler_params=pltpu.CompilerParams(vmem_limit_bytes=60 << 20),
        cost_estimate=pl.CostEstimate(
            flops=0, bytes_accessed=0, transcendentals=0
        ),
        name=f"stage{stage}",
    )(table, counts, packed, *operands)


def packed_lists(a_index, b_index, c_index, pair_count):
    position = lax.broadcasted_iota(jnp.int32, a_index.shape, 1)
    target = jnp.where(position < pair_count[:, None], c_index, SLOTS_C)
    return a_index | (b_index << B_SHIFT) | (target << C_SHIFT)


def shifted(value, axis, steps):
    count = lax.axis_size(axis)
    return lax.ppermute(value, axis, [(source, (source + steps) % count) for source in range(count)])


def any_mesh(a_blocks, b_blocks, a_index, b_index, c_index, pair_count):
    row, col = lax.axis_index("row"), lax.axis_index("col")
    rows, cols = lax.axis_size("row"), lax.axis_size("col")
    ticks = a_index.shape[2]
    back = ticks // 2 - 1
    counts = pair_count[0, 0]
    packed = packed_lists(a_index[0, 0], b_index[0, 0], c_index[0, 0], counts)
    a_now = shifted(a_blocks[0, 0], "row", back)
    b_now = shifted(b_blocks[0, 0], "col", back)
    halves = b_now.shape[0]
    running = None
    for tick in range(ticks):
        half = (row + col + tick - back) % rows // cols
        entry = jnp.concatenate(
            [jnp.array([1, tick, 0], jnp.int32), half[None].astype(jnp.int32), jnp.zeros((FIELDS - 4,), jnp.int32)]
        )
        running = run_stage(
            0, entry, counts, packed, [a_now, b_now],
            {0: (0,)}, {h: (1, h) for h in range(halves)},
            running, tick == ticks - 1, packed.shape[1],
        )
        if tick < ticks - 1:
            a_now = shifted(a_now, "row", -1)
            b_now = shifted(b_now, "col", -1)
    return running[None, None]


ROWS, COLS = 8, 4
OWN, OUTER, INNER, SECOND, INNER_FAR, THIRD = range(6)
A_STAGE = (0, 0, 0, 0, 0, 0, 0, 0)
B_STAGE = ((0, 0), (0, 0), (0, 0), (0, 0), (0, 0), (0, 1))
STAGES = 2


def a_place(row, target):
    delta = row ^ target
    by_core, hop = delta & 1, delta & 6
    if hop in (0, 6):
        return hop + by_core
    return (2 if (hop == 2) == ((row & 1) == by_core) else 4) + by_core


def b_source(col, target):
    if target == col:
        return OWN
    if col in (0, 3):
        return (None, OUTER, SECOND, THIRD)[abs(target - col)]
    if abs(target - col) == 2:
        return INNER_FAR
    return OUTER if target in (0, 3) else INNER


def stage_tables(ticks=8):
    tables = np.zeros((ROWS, COLS, STAGES, FIELDS), np.int32)
    for row in range(ROWS):
        for col in range(COLS):
            lists = [[] for _ in range(STAGES)]
            for tick in range(ticks):
                offset = tick - (ticks // 2 - 1)
                place = a_place(row, (row + offset) % ROWS)
                source = b_source(col, (col + offset) % COLS)
                half = (row + col + offset) % ROWS // COLS
                ready = max(A_STAGE[place], B_STAGE[source][half])
                lists[ready].append((tick, place, 2 * source + half))
            for stage, entries in enumerate(lists):
                tables[row, col, stage, 0] = len(entries)
                for k, entry in enumerate(entries):
                    tables[row, col, stage, 1 + 3 * k : 4 + 3 * k] = entry
    return tables


def used(tables, stage, field):
    found = set()
    for entries in tables[:, :, stage].reshape(-1, FIELDS):
        found |= {int(entries[field + 3 * k]) for k in range(entries[0])}
    return sorted(found)


def sent(name, value, place_of):
    pairs = []
    for row in range(ROWS):
        for col in range(COLS):
            to_row, to_col = place_of(row, col)
            pairs.append((COLS * row + col, COLS * to_row + to_col))
    with jax.named_scope(name):
        return lax.ppermute(value, ("row", "col"), pairs)


def after(value, *others):
    return lax.optimization_barrier((value, *others))[0]


def outward(value, name):
    return sent(name, value, lambda row, col: (row, col ^ 1))


def inward(value, name):
    return sent(name, value, lambda row, col: (row, 3 - col) if col in (1, 2) else (row ^ 1, col))


def second_over(value, name):
    return sent(name, value, lambda row, col: (row ^ 1, (2, 0, 3, 1)[col]) if col in (0, 3) else (row, (2, 0, 3, 1)[col]))


def end_to_end(value, name):
    return sent(name, value, lambda row, col: (row, 3 - col) if col in (0, 3) else (row ^ 1, col))


def swapped(value, name):
    return sent(name, value, lambda row, col: (row ^ 1, col))


def across(value, bits, name):
    return sent(name, value, lambda row, col: (row ^ bits, col))


def ax(value, name):
    return across(value, 2, name)


def ay(value, name):
    return across(value, 4, name)


def first_hop(value, name):
    return sent(name, value, lambda row, col: (row ^ (4 if row & 1 else 2), col))


def second_hop(value, name):
    return sent(name, value, lambda row, col: (row ^ (2 if row & 1 else 4), col))


def block_mesh(a_blocks, b_blocks, a_index, b_index, c_index, pair_count):
    row, col = lax.axis_index("row"), lax.axis_index("col")
    counts = pair_count[0, 0]
    packed = packed_lists(a_index[0, 0], b_index[0, 0], c_index[0, 0], counts)
    tables = stage_tables(a_index.shape[2])
    table = jnp.asarray(tables)[row, col].reshape(-1)
    a_own, b_own = a_blocks[0, 0], b_blocks[0, 0]
    def stage_call(stage, total):
        arrays, a_views, b_views = [], {}, {}

        def number_of(value):
            for number, held in enumerate(arrays):
                if held is value:
                    return number
            arrays.append(value)
            return len(arrays) - 1

        for place in used(tables, stage, 2):
            a_views[place] = tuple(number_of(value) for value in a_at[place])
        for source in used(tables, stage, 3):
            value, half = b_at[source]
            b_views[source] = (number_of(value), half)
        return run_stage(stage, table, counts, packed, arrays, a_views, b_views, total, stage == STAGES - 1, 150)

    O = outward(b_own, "O")
    I = inward(b_own, "I")
    H1 = first_hop(a_own, "H1")
    H2 = second_hop(a_own, "H2")
    W0 = swapped(a_own, "W0")
    S0 = outward(I[0], "S0")
    F0 = inward(after(O, W0, packed, table)[0], "F0")
    S1 = outward(I[1], "S1")
    F1 = inward(O[1], "F1")
    Ha = second_hop(H1[:32], "Ha")
    Hb = second_hop(H1[32:], "Hb")
    W1 = swapped(after(H1, S0, S1), "W1")
    T0 = outward(F0, "T0")
    W3 = swapped(Ha, "W3")
    W4 = swapped(Hb, "W4")
    W2 = swapped(after(H2, S0, S1), "W2")
    T1 = outward(after(F1, S0), "T1")
    a_at = [(a_own,), (W0,), (H1,), (W1,), (H2,), (W2,), (Ha, Hb), (W3, W4)]
    b_at = [(b_own, 0), (b_own, 1), (O, 0), (O, 1), (I, 0), (I, 1)]
    b_at += [(value, None) for value in (S0, S1, F0, F1, T0, T1)]
    total = None
    for stage in range(STAGES):
        total = stage_call(stage, total)
    return total[None, None]


def solution(mesh):
    placed = (
        P("row", "col", None, None, None),
        P("row", "col", None, None, None, None),
        P("row", "col", None, None),
        P("row", "col", None, None),
        P("row", "col", None, None),
        P("row", "col", None),
    )
    exact = (mesh.shape["row"], mesh.shape["col"]) == (ROWS, COLS)
    return jax.shard_map(
        block_mesh if exact else any_mesh,
        mesh=mesh,
        in_specs=placed,
        out_specs=P("row", "col", None, None, None),
        check_vma=False,
    )
```
